32 devices in a mesh: gx: 8 (over z, core), gy: 4 (over y, x).
Axes of the slice: x: 2, y: 2, z: 4, core: 2. Of those that a mesh axis runs over, the one named last changes fastest.
Arguments:
- blocks: bfloat16 [8, 4, 3, 320, 2240], P('gx', 'gy'), may hold values from -1 to 2
- right_side: bfloat16 [8, 4, 3, 320, 128], P('gx', 'gy'), may hold values from -6 to 6
- departure: int32 [8, 4, 2], P('gx', 'gy'), may hold values from -1 to 2, as said below
- arrival: int32 [8, 4, 2], P('gx', 'gy'), may hold values from 0 to 4, as said below
- neighbors: int32 [8, 4, 2, 6], P('gx', 'gy'), may hold values from 0 to 5, as said below
- orientation: int32 [8, 4, 2, 6], P('gx', 'gy'), may hold values from 0 to 3
Outputs:
- smoothed: float32 [8, 4, 2, 320, 128], P('gx', 'gy')
The draws below stay inside these ranges and needn't reach their ends.
Inputs may be any that keep to these rules, and one draw needn't show every extreme that they name: Position (l, c) holds its rows in some of its 3 slots; its live slots are exactly those named in its departure or arrival entries, each once. At most one of the two entries is a slot; the device with c = 0 never sends lower, the one with c = 3 never upper. Every position holds 1 to 3 rows before and exactly 2 after; in every layer some position holds 3. `arrival`: values below 3 name a local slot, kept in rising order; 3 is the row that the lower gy neighbour sends upward, 4 the one the upper neighbour sends downward, consistent with departure. `neighbors`: face 0 names 0 or 1, face 1 names 4 or 5; no entry of row q names 2 + q.
All inputs are finite; a program needn't handle non-finite values.
Results may differ from the reference program's by a relative error of at most 0.0035.
Values may be sent and summed in bfloat16 or wider, within the bound.
A program may use at most 64 MiB of HBM per device.

```python
import math
import jax
import jax.numpy as jnp
from jax import lax

VARS = 5
NODES = 4
DOF = 320
FACES = 6
SLOTS = 3
KEPT = 2
RHS = 128
ITERS = 4
LAYERS = 8
COLUMNS = 4


def balance_plan(key):
    sign_key, moving_key, forced_key, slot_key = jax.random.split(jax.random.fold_in(key, 7), 4)
    edge_shape = (LAYERS, COLUMNS - 1)
    signs = 2 * jax.random.randint(sign_key, edge_shape, 0, 2) - 1
    moving = jax.random.randint(moving_key, edge_shape, 0, 2)
    forced = jax.random.randint(forced_key, (LAYERS, 1), 0, COLUMNS - 1)
    edges = jnp.arange(COLUMNS - 1, dtype=jnp.int32)[None, :]
    signs = jnp.where(edges == forced, 1, signs)
    moving = jnp.where(edges == forced, 1, jnp.where(edges == forced - 1, 0, moving))
    flows = signs * moving
    earlier = jnp.pad(flows[:, :-1], ((0, 0), (1, 0)))
    flows = jnp.where(earlier * flows < 0, 0, flows)
    upper_edge = jnp.pad(flows, ((0, 0), (0, 1)))
    lower_edge = jnp.pad(flows, ((0, 0), (1, 0)))
    out_upper = (upper_edge == 1).astype(jnp.int32)
    out_lower = (lower_edge == -1).astype(jnp.int32)
    in_lower = (lower_edge == 1).astype(jnp.int32)
    in_upper = (upper_edge == -1).astype(jnp.int32)
    live_count = 2 + out_upper + out_lower - in_lower - in_upper
    leaving = jax.random.randint(slot_key, (LAYERS, COLUMNS), 0, live_count)
    departs = out_lower + out_upper
    departure = jnp.stack([jnp.where(out_lower > 0, leaving, -1), jnp.where(out_upper > 0, leaving, -1)], axis=-1)
    kept_count = live_count - departs
    slot_ids = jnp.arange(KEPT, dtype=jnp.int32)[None, None, :]
    local = jnp.where((departs[..., None] > 0) & (slot_ids >= leaving[..., None]), slot_ids + 1, slot_ids)
    incoming = jnp.where(in_lower > 0, SLOTS, SLOTS + 1)[..., None]
    arrival = jnp.where(slot_ids < kept_count[..., None], local, incoming)
    return (departure.astype(jnp.int32), arrival.astype(jnp.int32))


def draw_departure(key, part):
    return balance_plan(key)[0]


def draw_arrival(key, part):
    return balance_plan(key)[1]


def draw_neighbors(key, part):
    lower_key, upper_key, other_key = jax.random.split(jax.random.fold_in(key, 11), 3)
    lower = jax.random.randint(lower_key, (LAYERS, COLUMNS, KEPT, 1), 0, 2)
    upper = 4 + jax.random.randint(upper_key, (LAYERS, COLUMNS, KEPT, 1), 0, 2)
    others = jax.random.randint(other_key, (LAYERS, COLUMNS, KEPT, FACES - 2), 0, 5)
    itself = 2 + jnp.arange(KEPT, dtype=jnp.int32)[None, None, :, None]
    others = others + (others >= itself).astype(jnp.int32)
    return jnp.concatenate([lower, upper, others], axis=-1).astype(jnp.int32)


def draw_blocks(key, part):
    shape = (LAYERS, COLUMNS, SLOTS, DOF, 7 * DOF)
    noise_key = jax.random.fold_in(jax.random.fold_in(key, 3), 0)
    column_ids = jnp.arange(7 * DOF)[None, :]
    row_ids = jnp.arange(DOF)[:, None]
    spread = jnp.where(column_ids < DOF, 0.3, 0.15) / math.sqrt(DOF)
    noise = jax.random.normal(noise_key, shape, jnp.float32)
    identity = (column_ids == row_ids).astype(jnp.float32)
    return (identity + spread * noise).astype(jnp.bfloat16)


def set_ends(entries, key, least, high):
    dims = entries.shape
    spot = [jax.random.randint(jax.random.fold_in(key, axis), (), 0, dims[axis]) for axis in range(len(dims))]
    entries = entries.at[tuple(spot)].set(least)
    longest = dims.index(max(dims))
    spot[longest] = (spot[longest] + 1) % dims[longest]
    return entries.at[tuple(spot)].set(high)


def block_levels(rng, shape, cuts, least, high):
    level, own = 1.0, jax.random.fold_in(rng, 6)
    for axis_at, blocks in cuts:
        draws = jnp.exp(jax.random.uniform(jax.random.fold_in(own, axis_at), (blocks,), jnp.float32, least / len(cuts), high / len(cuts)))
        level = level * jnp.repeat(draws, shape[axis_at] // blocks).reshape([-1 if axis == axis_at else 1 for axis in range(len(shape))])
    return level


def normal_values(stream_key, shape, deviation, most, cuts=(), kind=jnp.bfloat16):
    values = deviation * jax.random.normal(stream_key, shape, jnp.float32)
    if cuts:
        values = values * block_levels(stream_key, shape, cuts, -0.22, 0.18)
    return jnp.clip(values, -most, most).astype(kind)


def setup_inputs(seed: int = 0) -> dict:
    arg_keys = jax.random.split(jax.random.key(seed), 7)
    blocks = draw_blocks(jax.random.fold_in(arg_keys[6], 71), 0)
    right_side = normal_values(arg_keys[1], (LAYERS, COLUMNS, SLOTS, DOF, RHS), 1.0, 6.0, ((0, 8), (1, 4)))
    departure = draw_departure(jax.random.fold_in(arg_keys[6], 71), 0)
    arrival = draw_arrival(jax.random.fold_in(arg_keys[6], 71), 0)
    neighbors = draw_neighbors(jax.random.fold_in(arg_keys[6], 71), 0)
    orientation = set_ends(jax.random.randint(arg_keys[5], (LAYERS, COLUMNS, KEPT, FACES), 0, 4), jax.random.fold_in(arg_keys[5], 1), 0, 3).astype(jnp.int32)
    return dict(blocks=blocks, right_side=right_side, departure=departure, arrival=arrival, neighbors=neighbors, orientation=orientation)


RELAXATION = 0.7


def turned_faces(faces, face_codes):
    nodal = faces.reshape(faces.shape[:-2] + (VARS, NODES, NODES, NODES, faces.shape[-1]))
    result = nodal
    for quarter in range(1, 4):
        picked = (face_codes == quarter).reshape(face_codes.shape + (1, 1, 1, 1, 1))
        result = jnp.where(picked, jnp.rot90(nodal, quarter, axes=(-4, -3)), result)
    return result.reshape(faces.shape)


def reference(blocks, right_side, departure, arrival, neighbors, orientation):
    layers = arrival.shape[0]
    columns = arrival.shape[1]
    column_ids = jnp.arange(columns, dtype=jnp.int32)
    from_lower_slot = jnp.roll(departure[:, :, 1], 1, axis=1)[:, :, None]
    from_upper_slot = jnp.roll(departure[:, :, 0], -1, axis=1)[:, :, None]
    source_column = column_ids[None, :, None] + (arrival == SLOTS + 1).astype(jnp.int32) - (arrival == SLOTS).astype(jnp.int32)
    source_slot = jnp.where(arrival < SLOTS, arrival, jnp.where(arrival == SLOTS, from_lower_slot, from_upper_slot))
    layer_ids = jnp.arange(layers, dtype=jnp.int32)[:, None, None]
    row_rhs = right_side[layer_ids, source_column, source_slot].astype(jnp.float32)
    iterate = RELAXATION * row_rhs
    for sweep_index in range(ITERS):
        rounded = iterate.astype(jnp.bfloat16)
        padded = jnp.pad(rounded, ((1, 1), (0, 0), (0, 0), (0, 0), (0, 0)))

        def layer_image(layer_number):
            window = lax.dynamic_slice_in_dim(padded, layer_number, 3, 0)
            window = jnp.moveaxis(window, 1, 0).reshape(columns, 3 * KEPT, DOF, RHS)
            layer_rows = blocks[layer_number][source_column[layer_number], source_slot[layer_number]]
            faces = window[column_ids[:, None, None], neighbors[layer_number]]
            faces = turned_faces(faces, orientation[layer_number])
            stacked = jnp.concatenate([rounded[layer_number][:, :, None], faces], axis=2)
            stacked = stacked.reshape(columns, KEPT, 7 * DOF, RHS).astype(jnp.float32)
            return jnp.einsum("cqde,cqer->cqdr", layer_rows.astype(jnp.float32), stacked, precision=lax.Precision.HIGHEST)

        applied = lax.map(layer_image, jnp.arange(layers, dtype=jnp.int32))
        iterate = iterate + RELAXATION * (row_rhs - applied)
    return iterate
```

```python
import functools
import jax
import jax.numpy as jnp
from jax import lax
from jax.experimental import pallas as pl
from jax.experimental.pallas import tpu as pltpu
from jax.sharding import PartitionSpec as P

NODES = 4
ITERS = 4
RELAXATION = 0.7
CHUNK = 32
TILE = 256
MESH = pl.DeviceIdType.MESH


def spans(width):
    return [(start, min(TILE, width - start)) for start in range(0, width, TILE)]


def turn_matrix(start, width, dof, codes):
    row = lax.broadcasted_iota(jnp.int32, (width, width), 0)
    col = lax.broadcasted_iota(jnp.int32, (width, width), 1)
    plane = NODES * NODES
    a = (row // plane) % NODES
    b = (row // NODES) % NODES
    rest = row - a * plane - b * NODES
    first, last = start // dof, (start + width - 1) // dof
    code = jnp.full((width, width), codes[first], jnp.int32)
    for segment in range(first + 1, last + 1):
        code = jnp.where(row < segment * dof - start, code, codes[segment])
    top = NODES - 1
    turned_a = jnp.where(code == 0, a, jnp.where(code == 1, b, jnp.where(code == 2, top - a, top - b)))
    turned_b = jnp.where(code == 0, b, jnp.where(code == 1, top - a, jnp.where(code == 2, top - b, a)))
    source = rest + turned_a * plane + turned_b * NODES
    return jnp.where(source == col, 1.0, 0.0).astype(jnp.bfloat16)


def kernel(layers, columns, blocks, rhs, departure, arrival, neighbors, orientation, out,
           local, local_rhs, leaving, leaving_rhs, near, near_rhs, far, far_rhs,
           kept, turns, stacked, current, kept_rhs, *rest):
    windows, sems = rest[:ITERS], rest[ITERS:]
    (load_sem, load_rhs_sem, near_send, near_recv, far_send, far_recv, rhs_send, rhs_recv,
     first_send, first_recv, halo_send, halo_recv) = sems
    slots, dof, width = local.shape
    rows = kept.shape[0]
    faces = width // dof - 1
    count = dof // CHUNK
    column, layer = lax.axis_index("gy"), lax.axis_index("gx")
    odd = lax.rem(column, 2)
    partner = column + 1 - 2 * odd
    onward = column + 2 - 4 * odd
    behind = column - 2 + 4 * odd
    has_onward = (onward >= 0) & (onward < columns)
    has_far = (behind >= 0) & (behind < columns)
    has_lower, has_upper = layer > 0, layer < layers - 1

    def part(index):
        return pl.ds(pl.multiple_of(index * CHUNK, CHUNK), CHUNK)

    def load(index):
        return pltpu.make_async_copy(blocks.at[:, part(index)], local.at[:, part(index)], load_sem.at[index])

    def send(source, target, send_sem, recv_sem, device):
        return pltpu.make_async_remote_copy(
            src_ref=source, dst_ref=target, send_sem=send_sem, recv_sem=recv_sem,
            device_id=device, device_id_type=MESH)

    def to_partner(index):
        return send(leaving.at[part(index)], near.at[part(index)], near_send.at[index], near_recv.at[index], {"gy": partner})

    def relay(index):
        return send(near.at[part(index)], far.at[part(index)], far_send.at[index], far_recv.at[index], {"gy": onward})

    rhs_to_partner = send(leaving_rhs, near_rhs, rhs_send.at[0], rhs_recv.at[0], {"gy": partner})
    rhs_relay = send(near_rhs, far_rhs, rhs_send.at[1], rhs_recv.at[1], {"gy": onward})

    def to_lower(source, target, send_sem, recv_sem):
        return send(source, target, send_sem, recv_sem, {"gx": layer - 1})

    def to_upper(source, target, send_sem, recv_sem):
        return send(source, target, send_sem, recv_sem, {"gx": layer + 1})

    def halo_down(sweep, row):
        window = windows[sweep]
        return to_lower(window.at[rows + row], window.at[2 * rows + row],
                        halo_send.at[sweep, 0, row], halo_recv.at[sweep, 0, row])

    def halo_up(sweep, row):
        window = windows[sweep]
        return to_upper(window.at[rows + row], window.at[row],
                        halo_send.at[sweep, 1, row], halo_recv.at[sweep, 1, row])

    def first_down(index):
        window = windows[1]
        return to_lower(window.at[pl.ds(rows, rows), part(index)], window.at[pl.ds(2 * rows, rows), part(index)],
                        first_send.at[0, index], first_recv.at[0, index])

    def first_up(index):
        window = windows[1]
        return to_upper(window.at[pl.ds(rows, rows), part(index)], window.at[pl.ds(0, rows), part(index)],
                        first_send.at[1, index], first_recv.at[1, index])

    load_rhs = pltpu.make_async_copy(rhs, local_rhs, load_rhs_sem)
    load_rhs.start()

    @pl.loop(0, count)
    def _(index):
        load(index).start()

    barrier = pltpu.get_barrier_semaphore()
    pl.semaphore_signal(barrier, inc=1, device_id={"gy": partner}, device_id_type=MESH)
    others = ((has_onward, {"gy": onward}), (has_far, {"gy": behind}),
              (has_lower, {"gx": layer - 1}), (has_upper, {"gx": layer + 1}))
    expected = 1
    for present, device in others:
        expected = expected + jnp.where(present, 1, 0)

        @pl.when(present)
        def _():
            pl.semaphore_signal(barrier, inc=1, device_id=device, device_id_type=MESH)
    pl.semaphore_wait(barrier, expected)

    slot = jnp.maximum(jnp.maximum(departure[0, 0, 0], departure[0, 0, 1]), 0)

    def pick(index, choices):
        value = choices[-1]
        for number in range(len(choices) - 2, -1, -1):
            value = lax.select(index == number, choices[number], value)
        return value

    load_rhs.wait()
    leaving_rhs[...] = pick(slot, [local_rhs[s] for s in range(slots)])
    rhs_to_partner.start()

    @pl.loop(0, count)
    def _(index):
        load(index).wait()
        leaving[part(index)] = pick(slot, [local[s, part(index)] for s in range(slots)])
        to_partner(index).start()

    for edge, missing in ((0, layer == 0), (2 * rows, layer == layers - 1)):
        @pl.when(missing)
        def _():
            for window in windows:
                window[pl.ds(edge, rows)] = jnp.zeros((rows,) + window.shape[1:], window.dtype)

    rhs_to_partner.wait_recv()

    @pl.when(has_onward)
    def _():
        rhs_relay.start()

    @pl.loop(0, rows)
    def _(row):
        codes = [0] + [orientation[0, 0, row, face] for face in range(faces)]
        for number, (start, size) in enumerate(spans(width)):
            turns[row, number, :size, :size] = turn_matrix(start, size, dof, codes)

    @pl.when(has_far)
    def _():
        rhs_relay.wait_recv()

    def pool_index(row):
        source = arrival[0, 0, row]
        return jnp.where(source < slots, source, jnp.where(source == slots + 1 - odd, slots, slots + 1))

    for row in range(rows):
        value = pick(pool_index(row), [local_rhs[s] for s in range(slots)] + [near_rhs[...], far_rhs[...]])
        value = value.astype(jnp.float32)
        kept_rhs[row] = value
        value = RELAXATION * value
        current[row] = value
        windows[0][rows + row] = value.astype(jnp.bfloat16)

    @pl.when(has_lower)
    def _():
        for row in range(rows):
            halo_down(0, row).start()

    @pl.when(has_upper)
    def _():
        for row in range(rows):
            halo_up(0, row).start()

    def stack(sweep):
        window = windows[sweep]
        for row in range(rows):
            stacked[row, :dof] = window[rows + row]
            for face in range(faces):
                stacked[row, (face + 1) * dof:(face + 2) * dof] = window[neighbors[0, 0, row, face]]

    def halo_wait(sweep):
        @pl.when(has_lower)
        def _():
            for row in range(rows):
                halo_up(sweep, row).wait_recv()

        @pl.when(has_upper)
        def _():
            for row in range(rows):
                halo_down(sweep, row).wait_recv()

    def take(index):
        to_partner(index).wait_recv()

        @pl.when(has_onward)
        def _():
            relay(index).start()

    take(0)
    halo_wait(0)
    stack(0)

    def process(index):
        @pl.when(has_far)
        def _():
            relay(index).wait_recv()

        here = part(index)
        for row in range(rows):
            source = pool_index(row)
            for number, (start, size) in enumerate(spans(width)):
                lanes = slice(start, start + size)
                value = pick(source, [local[s, here, lanes] for s in range(slots)] + [near[here, lanes], far[here, lanes]])
                kept[row, here, lanes] = jnp.dot(
                    value, turns[row, number, :size, :size], preferred_element_type=jnp.float32).astype(jnp.bfloat16)
            applied = jnp.dot(kept[row, here], stacked[row], preferred_element_type=jnp.float32)
            value = current[row, here] + RELAXATION * (kept_rhs[row, here] - applied)
            current[row, here] = value
            windows[1][rows + row, here] = value.astype(jnp.bfloat16)

        @pl.when(has_lower)
        def _():
            first_down(index).start()

        @pl.when(has_upper)
        def _():
            first_up(index).start()

    @pl.loop(1, count)
    def _(index):
        take(index)
        process(index - 1)

    process(count - 1)

    @pl.loop(0, count)
    def _(index):
        @pl.when(has_lower)
        def _():
            first_up(index).wait_recv()

        @pl.when(has_upper)
        def _():
            first_down(index).wait_recv()

    for sweep in range(1, ITERS):
        if sweep > 1:
            halo_wait(sweep)
        stack(sweep)
        for row in range(rows):
            applied = jnp.dot(kept[row], stacked[row], preferred_element_type=jnp.float32)
            value = current[row] + RELAXATION * (kept_rhs[row] - applied)
            if sweep == ITERS - 1:
                out[row] = value
                continue
            current[row] = value
            windows[sweep + 1][rows + row] = value.astype(jnp.bfloat16)

            @pl.when(has_lower)
            def _():
                halo_down(sweep + 1, row).start()

            @pl.when(has_upper)
            def _():
                halo_up(sweep + 1, row).start()

    rhs_to_partner.wait_send()

    @pl.when(has_onward)
    def _():
        rhs_relay.wait_send()

    @pl.loop(0, count)
    def _(index):
        to_partner(index).wait_send()

        @pl.when(has_onward)
        def _():
            relay(index).wait_send()

        @pl.when(has_lower)
        def _():
            first_down(index).wait_send()

        @pl.when(has_upper)
        def _():
            first_up(index).wait_send()

    for sweep in range(ITERS):
        if sweep == 1:
            continue

        @pl.when(has_lower)
        def _():
            for row in range(rows):
                halo_down(sweep, row).wait_send()

        @pl.when(has_upper)
        def _():
            for row in range(rows):
                halo_up(sweep, row).wait_send()


def solution(mesh):
    layers, columns = mesh.shape["gx"], mesh.shape["gy"]
    assert columns % 2 == 0

    def step(blocks, right_side, departure, arrival, neighbors, orientation):
        slots, dof, width = blocks.shape[2:]
        many = right_side.shape[-1]
        rows = arrival.shape[-1]
        count = dof // CHUNK
        bf16, f32, dma = jnp.bfloat16, jnp.float32, pltpu.SemaphoreType.DMA
        scratch = [
            pltpu.VMEM((slots, dof, width), bf16),
            pltpu.VMEM((slots, dof, many), bf16),
            pltpu.VMEM((dof, width), bf16),
            pltpu.VMEM((dof, many), bf16),
            pltpu.VMEM((dof, width), bf16),
            pltpu.VMEM((dof, many), bf16),
            pltpu.VMEM((dof, width), bf16),
            pltpu.VMEM((dof, many), bf16),
            pltpu.VMEM((rows, dof, width), bf16),
            pltpu.VMEM((rows, len(spans(width)), TILE, TILE), bf16),
            pltpu.VMEM((rows, width, many), bf16),
            pltpu.VMEM((rows, dof, many), f32),
            pltpu.VMEM((rows, dof, many), f32),
        ]
        scratch += [pltpu.VMEM((3 * rows, dof, many), bf16) for _ in range(ITERS)]
        scratch += [
            dma((count,)), dma(()), dma((count,)), dma((count,)), dma((count,)), dma((count,)), dma((2,)), dma((2,)),
            dma((2, count)), dma((2, count)), dma((ITERS, 2, rows)), dma((ITERS, 2, rows)),
        ]
        smem = pl.BlockSpec(memory_space=pltpu.SMEM)
        out = pl.pallas_call(
            functools.partial(kernel, layers, columns),
            out_shape=jax.ShapeDtypeStruct((rows, dof, many), f32),
            in_specs=[pl.BlockSpec(memory_space=pl.ANY)] * 2 + [smem] * 4,
            out_specs=pl.BlockSpec(memory_space=pltpu.VMEM),
            scratch_shapes=scratch,
            compiler_params=pltpu.CompilerParams(collective_id=0, has_side_effects=True),
        )(blocks[0, 0], right_side[0, 0], departure, arrival, neighbors, orientation)
        return out[None, None]

    in_specs = (
        P("gx", "gy", None, None, None),
        P("gx", "gy", None, None, None),
        P("gx", "gy", None),
        P("gx", "gy", None),
        P("gx", "gy", None, None),
        P("gx", "gy", None, None),
    )
    return jax.shard_map(step, mesh=mesh, in_specs=in_specs,
                         out_specs=P("gx", "gy", None, None, None), check_vma=False)
```

```python
import functools
import jax
import jax.numpy as jnp
from jax import lax
from jax.experimental import pallas as pl
from jax.experimental.pallas import tpu as pltpu
from jax.sharding import PartitionSpec as P

NODES = 4
ITERS = 4
RELAXATION = 0.7
CHUNK = 16
GROUP = 2
TILE = 256
MESH = pl.DeviceIdType.MESH


def spans(width):
    return [(start, min(TILE, width - start)) for start in range(0, width, TILE)]


def halves(dof):
    block = NODES**3
    first = -(-(dof // block) // 2) * block
    return [(0, first), (first, dof - first)]


def turn_matrix(start, width, dof, codes):
    row = lax.broadcasted_iota(jnp.int32, (width, width), 0)
    col = lax.broadcasted_iota(jnp.int32, (width, width), 1)
    plane = NODES * NODES
    a = (row // plane) % NODES
    b = (row // NODES) % NODES
    rest = row - a * plane - b * NODES
    first, last = start // dof, (start + width - 1) // dof
    code = jnp.full((width, width), codes[first], jnp.int32)
    for segment in range(first + 1, last + 1):
        code = jnp.where(row < segment * dof - start, code, codes[segment])
    top = NODES - 1
    turned_a = jnp.where(code == 0, a, jnp.where(code == 1, b, jnp.where(code == 2, top - a, top - b)))
    turned_b = jnp.where(code == 0, b, jnp.where(code == 1, top - a, jnp.where(code == 2, top - b, a)))
    source = rest + turned_a * plane + turned_b * NODES
    return jnp.where(source == col, 1.0, 0.0).astype(jnp.bfloat16)


def kernel(layers, columns, blocks, rhs, departure, arrival, neighbors, orientation, out,
           local, local_rhs, leaving, leaving_rhs, near, near_rhs, far, far_rhs,
           turns, current, kept_rhs, partial, *rest):
    pieces = halves(local.shape[1])
    kept, stacked = rest[:2], rest[2:4]
    windows, sems = [rest[4 + 2 * sweep:6 + 2 * sweep] for sweep in range(ITERS)], rest[4 + 2 * ITERS:]
    (load_sem, load_rhs_sem, near_send, near_recv, far_send, far_recv, rhs_send, rhs_recv,
     first_send, first_recv, halo_send, halo_recv) = sems
    slots, dof, width = local.shape
    rows = current.shape[0]
    faces = width // dof - 1
    count = dof // CHUNK
    groups = count // GROUP
    tall = CHUNK * GROUP
    column, layer = lax.axis_index("gy"), lax.axis_index("gx")
    odd = lax.rem(column, 2)
    partner = column + 1 - 2 * odd
    onward = column + 2 - 4 * odd
    behind = column - 2 + 4 * odd
    has_onward = (onward >= 0) & (onward < columns)
    has_far = (behind >= 0) & (behind < columns)
    has_lower, has_upper = layer > 0, layer < layers - 1

    def part(index):
        return pl.ds(pl.multiple_of(index * CHUNK, CHUNK), CHUNK)

    def load(index):
        return pltpu.make_async_copy(blocks.at[:, part(index)], local.at[:, part(index)], load_sem.at[index])

    def send(source, target, send_sem, recv_sem, device):
        return pltpu.make_async_remote_copy(
            src_ref=source, dst_ref=target, send_sem=send_sem, recv_sem=recv_sem,
            device_id=device, device_id_type=MESH)

    def to_partner(index):
        return send(leaving.at[part(index)], near.at[part(index)], near_send.at[index], near_recv.at[index], {"gy": partner})

    def relay(index):
        return send(near.at[part(index)], far.at[part(index)], far_send.at[index], far_recv.at[index], {"gy": onward})

    rhs_to_partner = send(leaving_rhs, near_rhs, rhs_send.at[0], rhs_recv.at[0], {"gy": partner})
    rhs_relay = send(near_rhs, far_rhs, rhs_send.at[1], rhs_recv.at[1], {"gy": onward})

    def to_lower(source, target, send_sem, recv_sem):
        return send(source, target, send_sem, recv_sem, {"gx": layer - 1})

    def to_upper(source, target, send_sem, recv_sem):
        return send(source, target, send_sem, recv_sem, {"gx": layer + 1})

    own, low, high = pl.ds(rows, rows), pl.ds(0, rows), pl.ds(2 * rows, rows)

    def halo_down(sweep, piece):
        window = windows[sweep][piece]
        return to_lower(window.at[own], window.at[high], halo_send.at[sweep, 0, piece], halo_recv.at[sweep, 0, piece])

    def halo_up(sweep, piece):
        window = windows[sweep][piece]
        return to_upper(window.at[own], window.at[low], halo_send.at[sweep, 1, piece], halo_recv.at[sweep, 1, piece])

    def inside(piece, group):
        return pl.ds(pl.multiple_of(group * tall - pieces[piece][0], tall), tall)

    def first_down(piece, group):
        window, here = windows[1][piece], inside(piece, group)
        return to_lower(window.at[own, here], window.at[high, here], first_send.at[0, group], first_recv.at[0, group])

    def first_up(piece, group):
        window, here = windows[1][piece], inside(piece, group)
        return to_upper(window.at[own, here], window.at[low, here], first_send.at[1, group], first_recv.at[1, group])

    def both(down, up):
        @pl.when(has_lower)
        def _():
            down()

        @pl.when(has_upper)
        def _():
            up()

    load_rhs = pltpu.make_async_copy(rhs, local_rhs, load_rhs_sem)
    load_rhs.start()

    @pl.loop(0, count)
    def _(index):
        load(index).start()

    barrier = pltpu.get_barrier_semaphore()
    pl.semaphore_signal(barrier, inc=1, device_id={"gy": partner}, device_id_type=MESH)
    others = ((has_onward, {"gy": onward}), (has_far, {"gy": behind}),
              (has_lower, {"gx": layer - 1}), (has_upper, {"gx": layer + 1}))
    expected = 1
    for present, device in others:
        expected = expected + jnp.where(present, 1, 0)

        @pl.when(present)
        def _():
            pl.semaphore_signal(barrier, inc=1, device_id=device, device_id_type=MESH)
    pl.semaphore_wait(barrier, expected)

    slot = jnp.maximum(jnp.maximum(departure[0, 0, 0], departure[0, 0, 1]), 0)

    def pick(index, choices):
        value = choices[-1]
        for number in range(len(choices) - 2, -1, -1):
            value = lax.select(index == number, choices[number], value)
        return value

    load_rhs.wait()
    leaving_rhs[...] = pick(slot, [local_rhs[s] for s in range(slots)])
    rhs_to_partner.start()

    @pl.loop(0, count)
    def _(index):
        load(index).wait()
        leaving[part(index)] = pick(slot, [local[s, part(index)] for s in range(slots)])
        to_partner(index).start()

    for edge, missing in ((0, layer == 0), (2 * rows, layer == layers - 1)):
        @pl.when(missing)
        def _():
            for pair in windows:
                for window in pair:
                    window[pl.ds(edge, rows)] = jnp.zeros((rows,) + window.shape[1:], window.dtype)

    rhs_to_partner.wait_recv()

    @pl.when(has_onward)
    def _():
        rhs_relay.start()

    @pl.loop(0, rows)
    def _(row):
        codes = [0] + [orientation[0, 0, row, face] for face in range(faces)]
        for number, (start, size) in enumerate(spans(width)):
            turns[row, number, :size, :size] = turn_matrix(start, size, dof, codes)

    @pl.when(has_far)
    def _():
        rhs_relay.wait_recv()

    def pool_index(row):
        source = arrival[0, 0, row]
        return jnp.where(source < slots, source, jnp.where(source == slots + 1 - odd, slots, slots + 1))

    for row in range(rows):
        value = pick(pool_index(row), [local_rhs[s] for s in range(slots)] + [near_rhs[...], far_rhs[...]])
        value = value.astype(jnp.float32)
        kept_rhs[row] = value
        value = RELAXATION * value
        current[row] = value
        rounded = value.astype(jnp.bfloat16)
        for piece, (start, size) in enumerate(pieces):
            windows[0][piece][rows + row] = rounded[start:start + size]

    def halo_start(sweep, piece):
        both(lambda: halo_down(sweep, piece).start(), lambda: halo_up(sweep, piece).start())

    def halo_wait(sweep, piece):
        both(lambda: halo_up(sweep, piece).wait_recv(), lambda: halo_down(sweep, piece).wait_recv())

    def stack(sweep, piece):
        window, size = windows[sweep][piece], pieces[piece][1]
        for row in range(rows):
            stacked[piece][row, :size] = window[rows + row]
            for face in range(faces):
                stacked[piece][row, (face + 1) * size:(face + 2) * size] = window[neighbors[0, 0, row, face]]

    for piece in range(2):
        halo_start(0, piece)

    def take(index):
        to_partner(index).wait_recv()

        @pl.when(has_onward)
        def _():
            relay(index).start()

    def take_group(group):
        for member in range(GROUP):
            take(group * GROUP + member)

    take_group(0)
    for piece in range(2):
        halo_wait(0, piece)
        stack(0, piece)

    def process(piece, group):
        @pl.when(has_far)
        def _():
            for member in range(GROUP):
                relay(group * GROUP + member).wait_recv()

        here = pl.ds(pl.multiple_of(group * tall, tall), tall)
        for row in range(rows):
            source = pool_index(row)
            turned = []
            for number, (start, size) in enumerate(spans(width)):
                lanes = slice(start, start + size)
                value = pick(source, [local[s, here, lanes] for s in range(slots)] + [near[here, lanes], far[here, lanes]])
                turned.append(jnp.dot(
                    value, turns[row, number, :size, :size], preferred_element_type=jnp.float32).astype(jnp.bfloat16))
            turned = jnp.concatenate(turned, axis=1)
            applied = 0.0
            for part_of, (start, size) in enumerate(pieces):
                value = jnp.concatenate(
                    [turned[:, face * dof + start:face * dof + start + size] for face in range(faces + 1)], axis=1)
                kept[part_of][row, here] = value
                applied = applied + jnp.dot(value, stacked[part_of][row], preferred_element_type=jnp.float32)
            value = current[row, here] + RELAXATION * (kept_rhs[row, here] - applied)
            current[row, here] = value
            windows[1][piece][rows + row, inside(piece, group)] = value.astype(jnp.bfloat16)
        both(lambda: first_down(piece, group).start(), lambda: first_up(piece, group).start())

    for piece, (start, size) in enumerate(pieces):
        @pl.loop(start // tall, (start + size) // tall)
        def _(group):
            @pl.when(group + 1 < groups)
            def _():
                take_group(group + 1)
            process(piece, group)

    for sweep in range(1, ITERS):
        for piece, (start, size) in enumerate(pieces):
            if sweep > 1:
                halo_wait(sweep, piece)
            else:
                @pl.loop(start // tall, (start + size) // tall)
                def _(group):
                    both(lambda: first_up(piece, group).wait_recv(), lambda: first_down(piece, group).wait_recv())
            stack(sweep, piece)
            if piece == 0:
                for row in range(rows):
                    partial[row] = jnp.dot(kept[0][row], stacked[0][row], preferred_element_type=jnp.float32)
        for piece, (start, size) in enumerate(pieces):
            here = slice(start, start + size)
            for row in range(rows):
                applied = partial[row, here] + jnp.dot(
                    kept[1][row, here], stacked[1][row], preferred_element_type=jnp.float32)
                value = current[row, here] + RELAXATION * (kept_rhs[row, here] - applied)
                if sweep == ITERS - 1:
                    out[row, here] = value
                    continue
                current[row, here] = value
                windows[sweep + 1][piece][rows + row] = value.astype(jnp.bfloat16)
            if sweep < ITERS - 1:
                halo_start(sweep + 1, piece)

    rhs_to_partner.wait_send()

    @pl.when(has_onward)
    def _():
        rhs_relay.wait_send()

    @pl.loop(0, count)
    def _(index):
        to_partner(index).wait_send()

        @pl.when(has_onward)
        def _():
            relay(index).wait_send()

    for piece, (start, size) in enumerate(pieces):
        @pl.loop(start // tall, (start + size) // tall)
        def _(group):
            both(lambda: first_down(piece, group).wait_send(), lambda: first_up(piece, group).wait_send())

        for sweep in range(ITERS):
            if sweep != 1:
                both(lambda: halo_down(sweep, piece).wait_send(), lambda: halo_up(sweep, piece).wait_send())


def solution(mesh):
    layers, columns = mesh.shape["gx"], mesh.shape["gy"]
    assert columns % 2 == 0

    def step(blocks, right_side, departure, arrival, neighbors, orientation):
        slots, dof, width = blocks.shape[2:]
        many = right_side.shape[-1]
        rows = arrival.shape[-1]
        count = dof // CHUNK
        bf16, f32, dma = jnp.bfloat16, jnp.float32, pltpu.SemaphoreType.DMA
        scratch = [
            pltpu.VMEM((slots, dof, width), bf16),
            pltpu.VMEM((slots, dof, many), bf16),
            pltpu.VMEM((dof, width), bf16),
            pltpu.VMEM((dof, many), bf16),
            pltpu.VMEM((dof, width), bf16),
            pltpu.VMEM((dof, many), bf16),
            pltpu.VMEM((dof, width), bf16),
            pltpu.VMEM((dof, many), bf16),
            pltpu.VMEM((rows, len(spans(width)), TILE, TILE), bf16),
            pltpu.VMEM((rows, dof, many), f32),
            pltpu.VMEM((rows, dof, many), f32),
            pltpu.VMEM((rows, dof, many), f32),
        ]
        sizes = [size for _, size in halves(dof)]
        scratch += [pltpu.VMEM((rows, dof, width // dof * size), bf16) for size in sizes]
        scratch += [pltpu.VMEM((rows, width // dof * size, many), bf16) for size in sizes]
        scratch += [pltpu.VMEM((3 * rows, size, many), bf16) for _ in range(ITERS) for size in sizes]
        scratch += [
            dma((count,)), dma(()), dma((count,)), dma((count,)), dma((count,)), dma((count,)), dma((2,)), dma((2,)),
            dma((2, count // GROUP)), dma((2, count // GROUP)), dma((ITERS, 2, 2)), dma((ITERS, 2, 2)),
        ]
        smem = pl.BlockSpec(memory_space=pltpu.SMEM)
        out = pl.pallas_call(
            functools.partial(kernel, layers, columns),
            out_shape=jax.ShapeDtypeStruct((rows, dof, many), f32),
            in_specs=[pl.BlockSpec(memory_space=pl.ANY)] * 2 + [smem] * 4,
            out_specs=pl.BlockSpec(memory_space=pltpu.VMEM),
            scratch_shapes=scratch,
            compiler_params=pltpu.CompilerParams(collective_id=0, has_side_effects=True),
        )(blocks[0, 0], right_side[0, 0], departure, arrival, neighbors, orientation)
        return out[None, None]

    in_specs = (
        P("gx", "gy", None, None, None),
        P("gx", "gy", None, None, None),
        P("gx", "gy", None),
        P("gx", "gy", None),
        P("gx", "gy", None, None),
        P("gx", "gy", None, None),
    )
    return jax.shard_map(step, mesh=mesh, in_specs=in_specs,
                         out_specs=P("gx", "gy", None, None, None), check_vma=False)
```

```python
import functools
import jax
import jax.numpy as jnp
from jax import lax
from jax.experimental import pallas as pl
from jax.experimental.pallas import tpu as pltpu
from jax.sharding import PartitionSpec as P

NODES = 4
ITERS = 4
RELAXATION = 0.7
CHUNK = 16
GROUP = 2
TILE = 256
MESH = pl.DeviceIdType.MESH


def spans(width):
    return [(start, min(TILE, width - start)) for start in range(0, width, TILE)]


def halves(dof):
    block = NODES**3
    first = dof // block // 2 * block
    return [(0, first), (first, dof - first)]


def turn_matrix(start, width, dof, codes):
    row = lax.broadcasted_iota(jnp.int32, (width, width), 0)
    col = lax.broadcasted_iota(jnp.int32, (width, width), 1)
    plane = NODES * NODES
    a = (row // plane) % NODES
    b = (row // NODES) % NODES
    rest = row - a * plane - b * NODES
    first, last = start // dof, (start + width - 1) // dof
    code = jnp.full((width, width), codes[first], jnp.int32)
    for segment in range(first + 1, last + 1):
        code = jnp.where(row < segment * dof - start, code, codes[segment])
    top = NODES - 1
    turned_a = jnp.where(code == 0, a, jnp.where(code == 1, b, jnp.where(code == 2, top - a, top - b)))
    turned_b = jnp.where(code == 0, b, jnp.where(code == 1, top - a, jnp.where(code == 2, top - b, a)))
    source = rest + turned_a * plane + turned_b * NODES
    return jnp.where(source == col, 1.0, 0.0).astype(jnp.bfloat16)


def kernel(layers, columns, blocks, rhs, departure_in, arrival_in, neighbors_in, orientation_in, out,
           departure, arrival, neighbors, orientation,
           local, local_rhs, leaving, leaving_rhs, near, near_rhs, far, far_rhs,
           turns, current, kept_rhs, partial, *rest):
    pieces = halves(local.shape[1])
    kept, stacked = rest[:2], rest[2:4]
    windows, sems = [rest[4 + 2 * sweep:6 + 2 * sweep] for sweep in range(ITERS)], rest[4 + 2 * ITERS:]
    (load_sem, load_rhs_sem, near_send, near_recv, far_send, far_recv, rhs_send, rhs_recv,
     first_send, first_recv, halo_send, halo_recv, plan_sem) = sems
    slots, dof, width = local.shape
    rows = current.shape[0]
    faces = width // dof - 1
    count = dof // CHUNK
    groups = count // GROUP
    tall = CHUNK * GROUP
    column, layer = lax.axis_index("gy"), lax.axis_index("gx")
    odd = lax.rem(column, 2)
    partner = column + 1 - 2 * odd
    onward = column + 2 - 4 * odd
    behind = column - 2 + 4 * odd
    has_onward = (onward >= 0) & (onward < columns)
    has_far = (behind >= 0) & (behind < columns)
    has_lower, has_upper = layer > 0, layer < layers - 1

    def part(index):
        return pl.ds(pl.multiple_of(index * CHUNK, CHUNK), CHUNK)

    def load(index):
        return pltpu.make_async_copy(blocks.at[:, part(index)], local.at[:, part(index)], load_sem.at[index])

    def send(source, target, send_sem, recv_sem, device):
        return pltpu.make_async_remote_copy(
            src_ref=source, dst_ref=target, send_sem=send_sem, recv_sem=recv_sem,
            device_id=device, device_id_type=MESH)

    middle = -(-width // TILE) * TILE // 2
    sides = (slice(0, middle), slice(middle, width))

    def to_partner(index, side):
        here, lanes = part(index), sides[side]
        return send(leaving.at[here, lanes], near.at[here, lanes], near_send.at[side, index], near_recv.at[side, index], {"gy": partner})

    def relay(index, side):
        here, lanes = part(index), sides[side]
        return send(near.at[here, lanes], far.at[here, lanes], far_send.at[side, index], far_recv.at[side, index], {"gy": onward})

    rhs_to_partner = send(leaving_rhs, near_rhs, rhs_send.at[0], rhs_recv.at[0], {"gy": partner})
    rhs_relay = send(near_rhs, far_rhs, rhs_send.at[1], rhs_recv.at[1], {"gy": onward})

    def to_lower(source, target, send_sem, recv_sem):
        return send(source, target, send_sem, recv_sem, {"gx": layer - 1})

    def to_upper(source, target, send_sem, recv_sem):
        return send(source, target, send_sem, recv_sem, {"gx": layer + 1})

    own, low, high = pl.ds(rows, rows), pl.ds(0, rows), pl.ds(2 * rows, rows)

    def halo_down(sweep, piece):
        window = windows[sweep][piece]
        return to_lower(window.at[own], window.at[high], halo_send.at[sweep, 0, piece], halo_recv.at[sweep, 0, piece])

    def halo_up(sweep, piece):
        window = windows[sweep][piece]
        return to_upper(window.at[own], window.at[low], halo_send.at[sweep, 1, piece], halo_recv.at[sweep, 1, piece])

    def inside(piece, group):
        return pl.ds(pl.multiple_of(group * tall - pieces[piece][0], tall), tall)

    def first_down(piece, group):
        window, here = windows[1][piece], inside(piece, group)
        return to_lower(window.at[own, here], window.at[high, here], first_send.at[0, group], first_recv.at[0, group])

    def first_up(piece, group):
        window, here = windows[1][piece], inside(piece, group)
        return to_upper(window.at[own, here], window.at[low, here], first_send.at[1, group], first_recv.at[1, group])

    def both(down, up):
        @pl.when(has_lower)
        def _():
            down()

        @pl.when(has_upper)
        def _():
            up()

    load_rhs = pltpu.make_async_copy(rhs, local_rhs, load_rhs_sem)
    load_rhs.start()
    plans = [pltpu.make_async_copy(source, target, plan_sem.at[number]) for number, (source, target) in enumerate((
        (departure_in, departure), (arrival_in, arrival), (neighbors_in, neighbors), (orientation_in, orientation)))]
    for plan in plans:
        plan.start()

    @pl.loop(0, count)
    def _(index):
        load(index).start()

    barrier = pltpu.get_barrier_semaphore()
    pl.semaphore_signal(barrier, inc=1, device_id={"gy": partner}, device_id_type=MESH)
    others = ((has_onward, {"gy": onward}), (has_far, {"gy": behind}),
              (has_lower, {"gx": layer - 1}), (has_upper, {"gx": layer + 1}))
    expected = 1
    for present, device in others:
        expected = expected + jnp.where(present, 1, 0)

        @pl.when(present)
        def _():
            pl.semaphore_signal(barrier, inc=1, device_id=device, device_id_type=MESH)
    pl.semaphore_wait(barrier, expected)

    for plan in plans:
        plan.wait()
    slot = jnp.maximum(jnp.maximum(departure[0, 0, 0], departure[0, 0, 1]), 0)

    def pick(index, choices):
        value = choices[-1]
        for number in range(len(choices) - 2, -1, -1):
            value = lax.select(index == number, choices[number], value)
        return value

    load_rhs.wait()
    leaving_rhs[...] = pick(slot, [local_rhs[s] for s in range(slots)])
    rhs_to_partner.start()

    @pl.loop(0, count)
    def _(index):
        load(index).wait()
        leaving[part(index)] = pick(slot, [local[s, part(index)] for s in range(slots)])
        for side in range(2):
            to_partner(index, side).start()

    for edge, missing in ((0, layer == 0), (2 * rows, layer == layers - 1)):
        @pl.when(missing)
        def _():
            for pair in windows:
                for window in pair:
                    window[pl.ds(edge, rows)] = jnp.zeros((rows,) + window.shape[1:], window.dtype)

    rhs_to_partner.wait_recv()

    @pl.when(has_onward)
    def _():
        rhs_relay.start()

    @pl.loop(0, rows)
    def _(row):
        codes = [0] + [orientation[0, 0, row, face] for face in range(faces)]
        for number, (start, size) in enumerate(spans(width)):
            turns[row, number, :size, :size] = turn_matrix(start, size, dof, codes)

    @pl.when(has_far)
    def _():
        rhs_relay.wait_recv()

    def pool_index(row):
        source = arrival[0, 0, row]
        return jnp.where(source < slots, source, jnp.where(source == slots + 1 - odd, slots, slots + 1))

    for row in range(rows):
        value = pick(pool_index(row), [local_rhs[s] for s in range(slots)] + [near_rhs[...], far_rhs[...]])
        value = value.astype(jnp.float32)
        kept_rhs[row] = value
        value = RELAXATION * value
        current[row] = value
        rounded = value.astype(jnp.bfloat16)
        for piece, (start, size) in enumerate(pieces):
            windows[0][piece][rows + row] = rounded[start:start + size]

    def halo_start(sweep, piece):
        both(lambda: halo_down(sweep, piece).start(), lambda: halo_up(sweep, piece).start())

    def halo_wait(sweep, piece):
        both(lambda: halo_up(sweep, piece).wait_recv(), lambda: halo_down(sweep, piece).wait_recv())

    def stack(sweep, piece):
        window, size = windows[sweep][piece], pieces[piece][1]
        for row in range(rows):
            stacked[piece][row, :size] = window[rows + row]
            for face in range(faces):
                stacked[piece][row, (face + 1) * size:(face + 2) * size] = window[neighbors[0, 0, row, face]]

    for piece in range(2):
        halo_start(0, piece)

    def take(index):
        for side in range(2):
            to_partner(index, side).wait_recv()

            @pl.when(has_onward)
            def _():
                relay(index, side).start()

    def take_group(group):
        for member in range(GROUP):
            take(group * GROUP + member)

    take_group(0)
    for piece in range(2):
        halo_wait(0, piece)
        stack(0, piece)

    def process(piece, group):
        @pl.when(has_far)
        def _():
            for member in range(GROUP):
                for side in range(2):
                    relay(group * GROUP + member, side).wait_recv()

        here = pl.ds(pl.multiple_of(group * tall, tall), tall)
        for row in range(rows):
            source = pool_index(row)
            turned = []
            for number, (start, size) in enumerate(spans(width)):
                lanes = slice(start, start + size)
                value = pick(source, [local[s, here, lanes] for s in range(slots)] + [near[here, lanes], far[here, lanes]])
                turned.append(jnp.dot(
                    value, turns[row, number, :size, :size], preferred_element_type=jnp.float32).astype(jnp.bfloat16))
            turned = jnp.concatenate(turned, axis=1)
            applied = 0.0
            for part_of, (start, size) in enumerate(pieces):
                value = jnp.concatenate(
                    [turned[:, face * dof + start:face * dof + start + size] for face in range(faces + 1)], axis=1)
                kept[part_of][row, here] = value
                applied = applied + jnp.dot(value, stacked[part_of][row], preferred_element_type=jnp.float32)
            value = current[row, here] + RELAXATION * (kept_rhs[row, here] - applied)
            current[row, here] = value
            windows[1][piece][rows + row, inside(piece, group)] = value.astype(jnp.bfloat16)
        both(lambda: first_down(piece, group).start(), lambda: first_up(piece, group).start())

    for piece, (start, size) in enumerate(pieces):
        @pl.loop(start // tall, (start + size) // tall)
        def _(group):
            @pl.when(group + 1 < groups)
            def _():
                take_group(group + 1)
            process(piece, group)

    for sweep in range(1, ITERS):
        for piece, (start, size) in enumerate(pieces):
            if sweep > 1:
                halo_wait(sweep, piece)
            else:
                @pl.loop(start // tall, (start + size) // tall)
                def _(group):
                    both(lambda: first_up(piece, group).wait_recv(), lambda: first_down(piece, group).wait_recv())
            stack(sweep, piece)
            if piece == 0:
                for row in range(rows):
                    partial[row] = jnp.dot(kept[0][row], stacked[0][row], preferred_element_type=jnp.float32)
        for piece, (start, size) in enumerate(pieces):
            here = slice(start, start + size)
            for row in range(rows):
                applied = partial[row, here] + jnp.dot(
                    kept[1][row, here], stacked[1][row], preferred_element_type=jnp.float32)
                value = current[row, here] + RELAXATION * (kept_rhs[row, here] - applied)
                if sweep == ITERS - 1:
                    out[row, here] = value
                    continue
                current[row, here] = value
                windows[sweep + 1][piece][rows + row] = value.astype(jnp.bfloat16)
            if sweep < ITERS - 1:
                halo_start(sweep + 1, piece)

    rhs_to_partner.wait_send()

    @pl.when(has_onward)
    def _():
        rhs_relay.wait_send()

    @pl.loop(0, count)
    def _(index):
        for side in range(2):
            to_partner(index, side).wait_send()

            @pl.when(has_onward)
            def _():
                relay(index, side).wait_send()

    for piece, (start, size) in enumerate(pieces):
        @pl.loop(start // tall, (start + size) // tall)
        def _(group):
            both(lambda: first_down(piece, group).wait_send(), lambda: first_up(piece, group).wait_send())

        for sweep in range(ITERS):
            if sweep != 1:
                both(lambda: halo_down(sweep, piece).wait_send(), lambda: halo_up(sweep, piece).wait_send())


def solution(mesh):
    layers, columns = mesh.shape["gx"], mesh.shape["gy"]
    assert columns % 2 == 0

    def step(blocks, right_side, departure, arrival, neighbors, orientation):
        slots, dof, width = blocks.shape[2:]
        many = right_side.shape[-1]
        rows = arrival.shape[-1]
        count = dof // CHUNK
        bf16, f32, dma = jnp.bfloat16, jnp.float32, pltpu.SemaphoreType.DMA
        scratch = [pltpu.SMEM(plan.shape, plan.dtype) for plan in (departure, arrival, neighbors, orientation)]
        scratch += [
            pltpu.VMEM((slots, dof, width), bf16),
            pltpu.VMEM((slots, dof, many), bf16),
            pltpu.VMEM((dof, width), bf16),
            pltpu.VMEM((dof, many), bf16),
            pltpu.VMEM((dof, width), bf16),
            pltpu.VMEM((dof, many), bf16),
            pltpu.VMEM((dof, width), bf16),
            pltpu.VMEM((dof, many), bf16),
            pltpu.VMEM((rows, len(spans(width)), TILE, TILE), bf16),
            pltpu.VMEM((rows, dof, many), f32),
            pltpu.VMEM((rows, dof, many), f32),
            pltpu.VMEM((rows, dof, many), f32),
        ]
        sizes = [size for _, size in halves(dof)]
        scratch += [pltpu.VMEM((rows, dof, width // dof * size), bf16) for size in sizes]
        scratch += [pltpu.VMEM((rows, width // dof * size, many), bf16) for size in sizes]
        scratch += [pltpu.VMEM((3 * rows, size, many), bf16) for _ in range(ITERS) for size in sizes]
        scratch += [
            dma((count,)), dma(()), dma((2, count)), dma((2, count)), dma((2, count)), dma((2, count)), dma((2,)), dma((2,)),
            dma((2, count // GROUP)), dma((2, count // GROUP)), dma((ITERS, 2, 2)), dma((ITERS, 2, 2)), dma((4,)),
        ]
        out = pl.pallas_call(
            functools.partial(kernel, layers, columns),
            out_shape=jax.ShapeDtypeStruct((rows, dof, many), f32),
            in_specs=[pl.BlockSpec(memory_space=pl.ANY)] * 6,
            out_specs=pl.BlockSpec(memory_space=pltpu.VMEM),
            scratch_shapes=scratch,
            compiler_params=pltpu.CompilerParams(collective_id=0, has_side_effects=True),
        )(blocks[0, 0], right_side[0, 0], departure, arrival, neighbors, orientation)
        return out[None, None]

    in_specs = (
        P("gx", "gy", None, None, None),
        P("gx", "gy", None, None, None),
        P("gx", "gy", None),
        P("gx", "gy", None),
        P("gx", "gy", None, None),
        P("gx", "gy", None, None),
    )
    return jax.shard_map(step, mesh=mesh, in_specs=in_specs,
                         out_specs=P("gx", "gy", None, None, None), check_vma=False)
```
